32 devices in a mesh: groups: 2 (over y), span: 4 (over z), batch: 4 (over x, core).
Axes of the slice: x: 2, y: 2, z: 4, core: 2. Of those that a mesh axis runs over, the one named last changes fastest.
Arguments:
- embeddings: bfloat16 [8, 512, 768], P(('groups', 'batch'), 'span'), parts along dimension 0, may hold values from -3500 to 3500
- cluster_ids: int32 [8, 512], P(('groups', 'batch'), 'span'), parts along dimension 0, may hold values from 0 to 15, as said below
Outputs:
- nearest: float32 [8, 512], P(('groups', 'batch'), 'span'), parts along dimension 0
The draws below stay inside these ranges and needn't reach their ends.
There are 2 independent parts, one for each index of `groups`. The reference program is written for one: setup_inputs(seed, part) draws one part's arguments, and reference() takes and returns one part's arrays. A program takes and returns all parts, laid end to end along the dimension named above; each array names one. Nothing has to cross between parts.
Inputs may be any that keep to these rules, and one draw needn't show every extreme that they name: `cluster_ids`: on one device at most 96 rows carry ids of one residue modulo 4; in every batch some residue has exactly 96 rows on every device of the span.
All inputs are finite; a program needn't handle non-finite values.
Results may differ from the reference program's by a relative error of at most 0.00061.
Values may be sent and summed in bfloat16 or wider, within the bound.
No kernel may reach another device: no remote copies, remote signals or barrier semaphores. Data moves between devices by JAX's collectives and lax.ppermute only.
A program may use at most 64 MiB of HBM per device.

```python
import math
import jax
import jax.numpy as jnp
from jax import lax

D = 768
ROWS_DEV = 128
CLUS_DEV = 4
SPAN_DEVS = 4
BATCHES = 4
SPAN_ROWS = 512
CLUSTERS = 16
CAP = 96


def cluster_layout(key):
    heavy_owner = jax.random.randint(jax.random.fold_in(key, 11), (BATCHES,), 0, SPAN_DEVS)
    offsets = jax.random.randint(jax.random.fold_in(key, 12), (BATCHES, SPAN_DEVS), 0, SPAN_DEVS - 1)
    position = jnp.arange(ROWS_DEV, dtype=jnp.int32)
    others = (heavy_owner[:, None, None] + 1 + (position[None, None, :] - CAP + offsets[:, :, None]) % (SPAN_DEVS - 1)) % SPAN_DEVS
    owners = jnp.where(position[None, None, :] < CAP, heavy_owner[:, None, None], others)
    layers = jax.random.randint(jax.random.fold_in(key, 13), (BATCHES, SPAN_DEVS, ROWS_DEV), 0, CLUS_DEV)
    local_ids = owners + SPAN_DEVS * layers
    ranking = jax.random.randint(jax.random.fold_in(key, 14), (BATCHES, SPAN_DEVS, ROWS_DEV), 0, 1 << 20)
    shuffle = jnp.argsort(ranking * ROWS_DEV + position[None, None, :], axis=-1, stable=True)
    mixed = jnp.take_along_axis(local_ids, shuffle, axis=-1)
    return mixed.reshape(BATCHES, SPAN_ROWS).astype(jnp.int32)


def pick_rows(table, members):
    return table[members]


def draw_cluster_ids(key, part):
    return cluster_layout(key)


def draw_embeddings(key, part):
    members = cluster_layout(key)
    centres = jnp.clip(jax.random.normal(jax.random.fold_in(key, 21), (BATCHES, CLUSTERS, D), jnp.float32), -5.0, 5.0)
    picked = jax.vmap(pick_rows)(centres, members)
    jitter = jnp.clip(jax.random.normal(jax.random.fold_in(key, 22), (BATCHES, SPAN_ROWS, D), jnp.float32), -5.0, 5.0)
    spread = jnp.exp(jax.random.uniform(jax.random.fold_in(key, 23), (BATCHES, SPAN_ROWS, 1), jnp.float32, math.log(0.2), math.log(2.0)))
    columns = jnp.exp(jax.random.uniform(jax.random.fold_in(key, 24), (D,), jnp.float32, 0.0, math.log(10.0)))
    amplitude = jnp.exp(jax.random.uniform(jax.random.fold_in(key, 26), (BATCHES, SPAN_ROWS, 1), jnp.float32, 0.0, math.log(10.0)))
    return (amplitude * (picked + spread * jitter) * columns).astype(jnp.bfloat16)


def setup_inputs(seed: int = 0, part: int = 0) -> dict:
    seeds = jax.random.split(jax.random.key(seed), 3)
    part_keys = jax.random.split(jax.random.fold_in(seeds[2], part), 3)
    embeddings = draw_embeddings(jax.random.fold_in(jax.random.fold_in(seeds[2], part), 71), part)
    cluster_ids = draw_cluster_ids(jax.random.fold_in(jax.random.fold_in(seeds[2], part), 71), part)
    return {"embeddings": embeddings, "cluster_ids": cluster_ids}


def normalize(embeddings):
    values = embeddings.astype(jnp.float32)
    inverse = lax.rsqrt(lax.optimization_barrier(jnp.mean(values * values, axis=-1, keepdims=True)) + 1e-06)
    return (values * inverse * (1.0 / math.sqrt(values.shape[-1]))).astype(jnp.bfloat16)

def batch_nearest(normed, members):
    total_rows = normed.shape[0]
    block_count = total_rows // ROWS_DEV
    column_index = jnp.arange(total_rows, dtype=jnp.int32)

    def one_block(block_number):
        first_row = (block_number * ROWS_DEV).astype(jnp.int32)
        rows_block = lax.dynamic_slice_in_dim(normed, first_row, ROWS_DEV, 0)
        ids_block = lax.dynamic_slice_in_dim(members, first_row, ROWS_DEV, 0)
        scores = lax.dot_general(rows_block, normed, (((1,), (1,)), ((), ())), preferred_element_type=jnp.float32)
        row_index = first_row + jnp.arange(ROWS_DEV, dtype=jnp.int32)
        same_cluster = (ids_block[:, None] == members[None, :]) & (row_index[:, None] != column_index[None, :])
        return lax.optimization_barrier(jnp.max(jnp.where(same_cluster, scores, -1.0), axis=1))
    return lax.map(one_block, jnp.arange(block_count, dtype=jnp.int32)).reshape(total_rows)

def per_batch(inputs):
    return batch_nearest(inputs[0], inputs[1])

def reference(embeddings, cluster_ids):
    normed = normalize(embeddings)
    return lax.map(per_batch, (normed, cluster_ids))
```

```python
import math

import jax
import jax.numpy as jnp
from jax import lax
from jax.sharding import PartitionSpec as P


SPAN = "span"
BATCH = "batch"


def normalize(embeddings):
    values = embeddings.astype(jnp.float32)
    inverse = lax.rsqrt(jnp.mean(values * values, axis=-1, keepdims=True) + 1e-06)
    return (values * inverse * (1.0 / math.sqrt(values.shape[-1]))).astype(jnp.bfloat16)


def pair_scores(left, right):
    return lax.dot_general(
        left, right, (((1,), (1,)), ((), ())), preferred_element_type=jnp.float32
    )


def gathered(embeddings, cluster_ids):
    normed = normalize(embeddings[0])
    member_ids = cluster_ids[0]
    row_count = normed.shape[0]
    own_index = lax.axis_index(SPAN)
    own_rows = own_index * row_count + jnp.arange(row_count, dtype=jnp.int32)
    piece_rows = lax.all_gather(normed, SPAN, axis=0, tiled=True)
    piece_ids = lax.all_gather(member_ids.astype(jnp.bfloat16), SPAN, axis=0, tiled=True)
    scores = pair_scores(normed, piece_rows)
    column_rows = jnp.arange(piece_rows.shape[0], dtype=jnp.int32)
    same_cluster = (member_ids[:, None] == piece_ids.astype(jnp.int32)[None, :]) & (
        own_rows[:, None] != column_rows[None, :]
    )
    nearest = jnp.max(jnp.where(same_cluster, scores, -1.0), axis=1)
    return jnp.maximum(nearest, -1.0)[None, :]


TO_ROOT = (
    (("3e", "1e", "0e", "0o", "2o", "2e"), ("1o~",), ("3o~",)),
    (("2e", "1e", "1o", "2o"), ("0e", "0o"), ("3e", "3o")),
    (("0e", "1e", "1o", "0o"), ("3o", "2o", "2e", "3e")),
)
BACK = (
    (("1e", "0e", "0o", "1o"), ("2o", "3o", "3e", "2e")),
    (("1e", "3e", "2e", "2o", "0o", "0e"), ("1o~",), ("3o~",)),
    (("1e", "2e", "2o", "1o"), ("0e", "0o"), ("3e", "3o")),
)
SLOT = ((3, 0, 2, 1), (1, 2, 0, 3))
RETURN = ((0, 0, 2, 1), (1, 2, 0, 0))


def pairs(cycles, batches):
    moves = {}
    for stops in cycles:
        for here, there in zip(stops, stops[1:] + stops[:1]):
            for low in range(0, batches, 2):
                spot = (int(here[0]), low + "eo".index(here[1]))
                other = low ^ 2 if here.endswith("~") else low
                moves[spot] = (int(there[0]), other + "eo".index(there[1]))
    flat = lambda spot: spot[0] * batches + spot[1]
    return sorted((flat(a), flat(b)) for a, b in moves.items())


def at_root(batches):
    def per_device(embeddings, cluster_ids):
        rows = embeddings[0]
        row_count = rows.shape[0]
        axes = (SPAN, BATCH)
        routes = [pairs(cycles, batches) for cycles in TO_ROOT]
        arrived = [lax.ppermute(rows, axes, route) for route in routes]
        arrived_ids = [lax.ppermute(cluster_ids, axes, route) for route in routes]
        normed = jnp.concatenate([normalize(r) for r in [rows] + arrived], axis=0)
        ids = jnp.concatenate([cluster_ids] + arrived_ids, axis=1)[0]
        scores = pair_scores(normed, normed)
        index = jnp.arange(ids.shape[0], dtype=jnp.int32)
        keep = (ids[:, None] == ids[None, :]) & (index[:, None] != index[None, :])
        best = jnp.maximum(jnp.max(jnp.where(keep, scores, -1.0), axis=0), -1.0)
        best = best.reshape(-1, row_count)
        back = [lax.ppermute(best, axes, pairs(cycles, batches)) for cycles in BACK]
        place = lax.axis_index(SPAN)
        parity = lax.axis_index(BATCH) % 2
        slot = jnp.array(SLOT, jnp.int32)[parity, place]
        turn = jnp.array(RETURN, jnp.int32)[parity, place]
        result = jnp.where(turn == 0, back[0], jnp.where(turn == 1, back[1], back[2]))
        result = jnp.where(slot == 0, best, result)
        pick = jnp.arange(result.shape[0], dtype=jnp.int32)[:, None] == slot
        return jnp.max(jnp.where(pick, result, -1.0), axis=0)[None, :]

    return per_device


def solution(mesh):
    batches = mesh.shape[BATCH]
    line = mesh.shape[SPAN] == len(SLOT[0]) and batches % 4 == 0
    return jax.shard_map(
        at_root(batches) if line else gathered,
        mesh=mesh,
        in_specs=(P(("groups", BATCH), SPAN, None), P(("groups", BATCH), SPAN)),
        out_specs=P(("groups", BATCH), SPAN),
        check_vma=False,
    )
```

```python
import math

import jax
import jax.numpy as jnp
from jax import lax
from jax.sharding import PartitionSpec as P


SPAN = "span"
BATCH = "batch"


def normalize(embeddings):
    values = embeddings.astype(jnp.float32)
    inverse = lax.rsqrt(jnp.mean(values * values, axis=-1, keepdims=True) + 1e-06)
    return (values * inverse * (1.0 / math.sqrt(values.shape[-1]))).astype(jnp.bfloat16)


def pair_scores(left, right):
    return lax.dot_general(
        left, right, (((1,), (1,)), ((), ())), preferred_element_type=jnp.float32
    )


def gathered(embeddings, cluster_ids):
    normed = normalize(embeddings[0])
    member_ids = cluster_ids[0]
    row_count = normed.shape[0]
    own_index = lax.axis_index(SPAN)
    own_rows = own_index * row_count + jnp.arange(row_count, dtype=jnp.int32)
    piece_rows = lax.all_gather(normed, SPAN, axis=0, tiled=True)
    piece_ids = lax.all_gather(member_ids.astype(jnp.bfloat16), SPAN, axis=0, tiled=True)
    scores = pair_scores(normed, piece_rows)
    column_rows = jnp.arange(piece_rows.shape[0], dtype=jnp.int32)
    same_cluster = (member_ids[:, None] == piece_ids.astype(jnp.int32)[None, :]) & (
        own_rows[:, None] != column_rows[None, :]
    )
    nearest = jnp.max(jnp.where(same_cluster, scores, -1.0), axis=1)
    return jnp.maximum(nearest, -1.0)[None, :]


TO_ROOT = (
    (("3e", "1e", "0e", "0o", "2o", "2e"), ("1o~",), ("3o~",)),
    (("2e", "1e", "1o", "2o"), ("0e", "0o"), ("3e", "3o")),
    (("0e", "1e", "1o", "0o"), ("3o", "2o", "2e", "3e")),
)
BACK = (
    (("1e", "0e", "0o", "1o"), ("2o", "3o", "3e", "2e")),
    (("1e", "3e", "2e", "2o", "0o", "0e"), ("1o~",), ("3o~",)),
    (("1e", "2e", "2o", "1o"), ("0e", "0o"), ("3e", "3o")),
)
MEET = (1, 2)
PLACES = 4


def following(cycles, spot):
    for stops in cycles:
        names = [stop[:2] for stop in stops]
        if spot in names:
            return names[(names.index(spot) + 1) % len(names)]


def wanted(place, parity):
    spot, root = f"{place}{'eo'[parity]}", f"{MEET[parity]}{'eo'[parity]}"
    if spot == root:
        return 0
    block = 1 + [following(cycles, spot) == root for cycles in TO_ROOT].index(True)
    source = 1 + [following(cycles, root) == spot for cycles in BACK].index(True)
    return source * PLACES + block


def pairs(cycles, batches):
    moves = {}
    for stops in cycles:
        for here, there in zip(stops, stops[1:] + stops[:1]):
            for low in range(0, batches, 2):
                spot = (int(here[0]), low + "eo".index(here[1]))
                other = low ^ 2 if here.endswith("~") else low
                moves[spot] = (int(there[0]), other + "eo".index(there[1]))
    flat = lambda spot: spot[0] * batches + spot[1]
    return sorted((flat(a), flat(b)) for a, b in moves.items())


def travel(array, cycles, batches):
    return lax.ppermute(array, (SPAN, BATCH), pairs(cycles, batches))


def at_root(batches):
    def per_device(embeddings, cluster_ids):
        return whole(embeddings, cluster_ids)

    def whole(embeddings, cluster_ids):
        rows = embeddings[0]
        row_count = rows.shape[0]
        arrived = [travel(rows, cycles, batches) for cycles in TO_ROOT]
        arrived_ids = [travel(cluster_ids, cycles, batches) for cycles in TO_ROOT]
        normed = jnp.concatenate([normalize(r) for r in [rows] + arrived], axis=0)
        ids = jnp.concatenate([cluster_ids] + arrived_ids, axis=1)[0]
        scores = pair_scores(normed, normed)
        index = jnp.arange(ids.shape[0], dtype=jnp.int32)
        keep = (ids[:, None] == ids[None, :]) & (index[:, None] != index[None, :])
        best = jnp.maximum(jnp.max(jnp.where(keep, scores, -1.0), axis=0), -1.0)
        best = best.reshape(-1, row_count)
        back = [travel(best, cycles, batches) for cycles in BACK]
        stack = jnp.concatenate([best] + back, axis=0)
        where_am_i = lax.axis_index(SPAN) * 2 + (lax.axis_index(BATCH) & 1)
        row = lax.broadcasted_iota(jnp.int32, stack.shape, 0)
        mine = jnp.zeros(stack.shape, jnp.bool_)
        for place in range(PLACES):
            for parity in range(2):
                here = where_am_i == place * 2 + parity
                mine |= here & (row == wanted(place, parity))
        return jnp.max(jnp.where(mine, stack, -1.0), axis=0)[None, :]

    return per_device


def solution(mesh):
    batches = mesh.shape[BATCH]
    line = mesh.shape[SPAN] == PLACES and batches % 4 == 0
    return jax.shard_map(
        at_root(batches) if line else gathered,
        mesh=mesh,
        in_specs=(P(("groups", BATCH), SPAN, None), P(("groups", BATCH), SPAN)),
        out_specs=P(("groups", BATCH), SPAN),
        check_vma=False,
    )
```

```python
import math

import jax
import jax.numpy as jnp
from jax import lax
from jax.experimental import pallas as pl
from jax.experimental.pallas import tpu as pltpu
from jax.sharding import PartitionSpec as P


SPAN = "span"
BATCH = "batch"


def normalize(embeddings):
    values = embeddings.astype(jnp.float32)
    inverse = lax.rsqrt(jnp.mean(values * values, axis=-1, keepdims=True) + 1e-06)
    return (values * inverse * (1.0 / math.sqrt(values.shape[-1]))).astype(jnp.bfloat16)


def pair_scores(left, right):
    return lax.dot_general(
        left, right, (((1,), (1,)), ((), ())), preferred_element_type=jnp.float32
    )


def gathered(embeddings, cluster_ids):
    normed = normalize(embeddings[0])
    member_ids = cluster_ids[0]
    row_count = normed.shape[0]
    own_index = lax.axis_index(SPAN)
    own_rows = own_index * row_count + jnp.arange(row_count, dtype=jnp.int32)
    piece_rows = lax.all_gather(normed, SPAN, axis=0, tiled=True)
    piece_ids = lax.all_gather(member_ids.astype(jnp.bfloat16), SPAN, axis=0, tiled=True)
    scores = pair_scores(normed, piece_rows)
    column_rows = jnp.arange(piece_rows.shape[0], dtype=jnp.int32)
    same_cluster = (member_ids[:, None] == piece_ids.astype(jnp.int32)[None, :]) & (
        own_rows[:, None] != column_rows[None, :]
    )
    nearest = jnp.max(jnp.where(same_cluster, scores, -1.0), axis=1)
    return jnp.maximum(nearest, -1.0)[None, :]


TO_ROOT = (
    (("2e", "1e", "1o", "2o"), ("0e", "0o"), ("3e", "3o")),
    (("3e", "1e", "0e", "0o", "2o", "3o"), ("1o~",), ("2e~",)),
    (("0e", "1e", "1o", "0o"), ("3o", "2o", "2e", "3e")),
)
BACK = (
    (("1e", "0e", "0o", "1o"), ("2o", "3o", "3e", "2e")),
    (("1e", "3e", "2e", "2o", "0o", "0e"), ("1o~",), ("3o~",)),
    (("1e", "2e", "2o", "1o"), ("0e", "0o"), ("3e", "3o")),
)
MEET = (1, 2)
PLACES = 4


def following(cycles, spot):
    for stops in cycles:
        names = [stop[:2] for stop in stops]
        if spot in names:
            return names[(names.index(spot) + 1) % len(names)]


def wanted(place, parity):
    spot, root = f"{place}{'eo'[parity]}", f"{MEET[parity]}{'eo'[parity]}"
    if spot == root:
        return 0
    block = 1 + [following(cycles, spot) == root for cycles in TO_ROOT].index(True)
    source = 1 + [following(cycles, root) == spot for cycles in BACK].index(True)
    return source * PLACES + block


def pairs(cycles, batches):
    moves = {}
    for stops in cycles:
        for here, there in zip(stops, stops[1:] + stops[:1]):
            for low in range(0, batches, 2):
                spot = (int(here[0]), low + "eo".index(here[1]))
                other = low ^ 2 if here.endswith("~") else low
                moves[spot] = (int(there[0]), other + "eo".index(there[1]))
    flat = lambda spot: spot[0] * batches + spot[1]
    return sorted((flat(a), flat(b)) for a, b in moves.items())


def travel(array, cycles, batches):
    return lax.ppermute(array, (SPAN, BATCH), pairs(cycles, batches))


GRANT = pltpu.CompilerParams(vmem_limit_bytes=8 << 20)
WHOLE = pl.BlockSpec(memory_space=pltpu.VMEM)


def own_body(rows, out):
    out[...] = normalize(rows[...])


def root_body(own, *refs):
    n = PLACES
    arrived, ids, out = refs[: n - 1], refs[n - 1 : 2 * n - 1], refs[2 * n - 1]
    count = own.shape[0]
    normed = jnp.concatenate([own[...]] + [normalize(r[...]) for r in arrived], axis=0)
    across = jnp.concatenate([i[...] for i in ids], axis=1)
    index = lax.broadcasted_iota(jnp.int32, (1, across.shape[1]), 1)
    down = jnp.transpose(jnp.broadcast_to(across, (8, across.shape[1])))[:, :1]
    down_index = lax.broadcasted_iota(jnp.int32, (down.shape[0], 1), 0)
    scores = pair_scores(normed, normed)
    keep = (down == across) & (down_index != index)
    best = jnp.maximum(jnp.max(jnp.where(keep, scores, -1.0), axis=0, keepdims=True), -1.0)
    for k in range(n):
        out[k : k + 1, :] = best[:, k * count : (k + 1) * count]


def own_rows(rows):
    return pl.pallas_call(
        own_body,
        out_shape=jax.ShapeDtypeStruct(rows.shape, jnp.bfloat16),
        in_specs=[WHOLE],
        out_specs=WHOLE,
        compiler_params=GRANT,
        name="own_rows",
    )(rows)


def all_results(own, arrived, ids):
    return pl.pallas_call(
        root_body,
        out_shape=jax.ShapeDtypeStruct((PLACES, own.shape[0]), jnp.float32),
        in_specs=[WHOLE] * (2 * PLACES),
        out_specs=WHOLE,
        compiler_params=GRANT,
        name="all_results",
    )(own, *arrived, *ids)


def at_root(batches):
    def per_device(embeddings, cluster_ids):
        return whole(embeddings, cluster_ids)

    def whole(embeddings, cluster_ids):
        rows = embeddings[0]
        arrived = [travel(rows, cycles, batches) for cycles in TO_ROOT]
        arrived_ids = [travel(cluster_ids, cycles, batches) for cycles in TO_ROOT]
        best = all_results(own_rows(rows), arrived, [cluster_ids] + arrived_ids)
        back = [travel(best, cycles, batches) for cycles in BACK]
        stack = jnp.concatenate([best] + back, axis=0)
        where_am_i = lax.axis_index(SPAN) * 2 + (lax.axis_index(BATCH) & 1)
        row = lax.broadcasted_iota(jnp.int32, stack.shape, 0)
        mine = jnp.zeros(stack.shape, jnp.bool_)
        for place in range(PLACES):
            for parity in range(2):
                here = where_am_i == place * 2 + parity
                mine |= here & (row == wanted(place, parity))
        return jnp.max(jnp.where(mine, stack, -1.0), axis=0)[None, :]

    return per_device


def solution(mesh):
    batches = mesh.shape[BATCH]
    line = mesh.shape[SPAN] == PLACES and batches % 4 == 0
    return jax.shard_map(
        at_root(batches) if line else gathered,
        mesh=mesh,
        in_specs=(P(("groups", BATCH), SPAN, None), P(("groups", BATCH), SPAN)),
        out_specs=P(("groups", BATCH), SPAN),
        check_vma=False,
    )
```

```python
import math

import jax
import jax.numpy as jnp
from jax import lax
from jax.experimental import pallas as pl
from jax.experimental.pallas import tpu as pltpu
from jax.sharding import PartitionSpec as P


SPAN = "span"
BATCH = "batch"


def normalize(embeddings):
    values = embeddings.astype(jnp.float32)
    inverse = lax.rsqrt(jnp.mean(values * values, axis=-1, keepdims=True) + 1e-06)
    return (values * inverse * (1.0 / math.sqrt(values.shape[-1]))).astype(jnp.bfloat16)


def pair_scores(left, right):
    return lax.dot_general(
        left, right, (((1,), (1,)), ((), ())), preferred_element_type=jnp.float32
    )


def gathered(embeddings, cluster_ids):
    normed = normalize(embeddings[0])
    member_ids = cluster_ids[0]
    row_count = normed.shape[0]
    own_index = lax.axis_index(SPAN)
    own_rows = own_index * row_count + jnp.arange(row_count, dtype=jnp.int32)
    piece_rows = lax.all_gather(normed, SPAN, axis=0, tiled=True)
    piece_ids = lax.all_gather(member_ids.astype(jnp.bfloat16), SPAN, axis=0, tiled=True)
    scores = pair_scores(normed, piece_rows)
    column_rows = jnp.arange(piece_rows.shape[0], dtype=jnp.int32)
    same_cluster = (member_ids[:, None] == piece_ids.astype(jnp.int32)[None, :]) & (
        own_rows[:, None] != column_rows[None, :]
    )
    nearest = jnp.max(jnp.where(same_cluster, scores, -1.0), axis=1)
    return jnp.maximum(nearest, -1.0)[None, :]


MEET = ("1o", "2o")
PLACES = 4
SWAP = tuple((f"{place}e", f"{place}o") for place in range(PLACES))
TO_ROOT = (
    (("0e", "0o", "2o", "2e", "3o", "3e", "1o", "1e"),),
    (("0e", "0o"), ("1e~",), ("2e", "1o", "2o"), ("3e", "3o")),
    (("0e", "1o", "1e", "0o"), ("2e", "3o", "2o"), ("3e~",)),
)
BACK = (
    (("0e", "2e", "2o", "0o", "1e", "1o"), ("3e", "3o")),
    (("0e", "0o"), ("1e", "1o", "2e"), ("3e", "2o", "3o")),
    (("0e", "0o"), ("1e~",), ("2e", "2o", "1o", "3e", "3o")),
)


def following(cycles, spot):
    for stops in cycles:
        names = [stop[:2] for stop in stops]
        if spot in names:
            return names[(names.index(spot) + 1) % len(names)]


def wanted(place, parity):
    spot, root = f"{place}{'eo'[parity]}", MEET[parity]
    there = [following(cycles, spot) == root for cycles in TO_ROOT]
    back = [following(cycles, root) == spot for cycles in BACK + (SWAP,)]
    block = 1 + there.index(True) if True in there else 0
    source = 1 + back.index(True) if spot != root else 0
    return source * PLACES + block


def pairs(cycles, batches):
    moves = {}
    for stops in cycles:
        for here, there in zip(stops, stops[1:] + stops[:1]):
            for low in range(0, batches, 2):
                spot = (int(here[0]), low + "eo".index(here[1]))
                other = low ^ 2 if here.endswith("~") else low
                moves[spot] = (int(there[0]), other + "eo".index(there[1]))
    flat = lambda spot: spot[0] * batches + spot[1]
    return sorted((flat(a), flat(b)) for a, b in moves.items())


def travel(array, cycles, batches):
    return lax.ppermute(array, (SPAN, BATCH), pairs(cycles, batches))


GRANT = pltpu.CompilerParams(vmem_limit_bytes=8 << 20)
WHOLE = pl.BlockSpec(memory_space=pltpu.VMEM)


def first_body(guest, own, other, out):
    use_other = jnp.max(guest[...], axis=1, keepdims=True) > 0
    out[...] = normalize(jnp.where(use_other, other[...], own[...]))


def root_body(first, *refs):
    n = PLACES
    arrived, (guest, own_ids, *ids), out = refs[: n - 1], refs[n - 1 : -1], refs[-1]
    count = first.shape[0]
    first_ids = jnp.where(guest[...] > 0, ids[-1][...], own_ids[...])
    normed = jnp.concatenate([first[...]] + [normalize(r[...]) for r in arrived], axis=0)
    across = jnp.concatenate([first_ids] + [i[...] for i in ids[:-1]], axis=1)
    index = lax.broadcasted_iota(jnp.int32, (1, across.shape[1]), 1)
    down = jnp.transpose(jnp.broadcast_to(across, (8, across.shape[1])))[:, :1]
    down_index = lax.broadcasted_iota(jnp.int32, (down.shape[0], 1), 0)
    scores = pair_scores(normed, normed)
    keep = (down == across) & (down_index != index)
    best = jnp.maximum(jnp.max(jnp.where(keep, scores, -1.0), axis=0, keepdims=True), -1.0)
    for k in range(n):
        out[k : k + 1, :] = best[:, k * count : (k + 1) * count]


def first_rows(guest, own, other):
    return pl.pallas_call(
        first_body,
        out_shape=jax.ShapeDtypeStruct(own.shape, jnp.bfloat16),
        in_specs=[WHOLE] * 3,
        out_specs=WHOLE,
        compiler_params=GRANT,
        name="first_rows",
    )(guest, own, other)


def all_results(first, arrived, ids):
    return pl.pallas_call(
        root_body,
        out_shape=jax.ShapeDtypeStruct((PLACES, first.shape[0]), jnp.float32),
        in_specs=[WHOLE] * (1 + len(arrived) + len(ids)),
        out_specs=WHOLE,
        compiler_params=GRANT,
        name="all_results",
    )(first, *arrived, *ids)


def at_root(batches):
    def per_device(embeddings, cluster_ids):
        return whole(embeddings, cluster_ids)

    def whole(embeddings, cluster_ids):
        rows = embeddings[0]
        where_am_i = lax.axis_index(SPAN) * 2 + (lax.axis_index(BATCH) & 1)
        guest = where_am_i == int(MEET[0][0]) * 2 + "eo".index(MEET[0][1])
        guest = jnp.broadcast_to(guest.astype(jnp.int32), cluster_ids.shape)
        inward, outward = TO_ROOT + (SWAP,), BACK + (SWAP,)
        arrived = [travel(rows, c, batches) for c in inward]
        arrived_ids = [travel(cluster_ids, c, batches) for c in inward]
        first = first_rows(guest, rows, arrived[-1])
        best = all_results(first, arrived[:-1], [guest, cluster_ids] + arrived_ids)
        back = [travel(best, c, batches) for c in outward]
        stack = jnp.concatenate([best] + back, axis=0)
        row = lax.broadcasted_iota(jnp.int32, stack.shape, 0)
        mine = jnp.zeros(stack.shape, jnp.bool_)
        for place in range(PLACES):
            for parity in range(2):
                here = where_am_i == place * 2 + parity
                mine |= here & (row == wanted(place, parity))
        return jnp.max(jnp.where(mine, stack, -1.0), axis=0)[None, :]

    return per_device


def solution(mesh):
    batches = mesh.shape[BATCH]
    line = mesh.shape[SPAN] == PLACES and batches % 4 == 0
    return jax.shard_map(
        at_root(batches) if line else gathered,
        mesh=mesh,
        in_specs=(P(("groups", BATCH), SPAN, None), P(("groups", BATCH), SPAN)),
        out_specs=P(("groups", BATCH), SPAN),
        check_vma=False,
    )
```

```python
import math

import jax
import jax.numpy as jnp
from jax import lax
from jax.experimental import pallas as pl
from jax.experimental.pallas import tpu as pltpu
from jax.sharding import PartitionSpec as P


SPAN = "span"
BATCH = "batch"


def normalize(embeddings):
    values = embeddings.astype(jnp.float32)
    inverse = lax.rsqrt(jnp.mean(values * values, axis=-1, keepdims=True) + 1e-06)
    return (values * inverse * (1.0 / math.sqrt(values.shape[-1]))).astype(jnp.bfloat16)


def pair_scores(left, right):
    return lax.dot_general(
        left, right, (((1,), (1,)), ((), ())), preferred_element_type=jnp.float32
    )


def gathered(embeddings, cluster_ids):
    normed = normalize(embeddings[0])
    member_ids = cluster_ids[0]
    row_count = normed.shape[0]
    own_index = lax.axis_index(SPAN)
    own_rows = own_index * row_count + jnp.arange(row_count, dtype=jnp.int32)
    piece_rows = lax.all_gather(normed, SPAN, axis=0, tiled=True)
    piece_ids = lax.all_gather(member_ids.astype(jnp.bfloat16), SPAN, axis=0, tiled=True)
    scores = pair_scores(normed, piece_rows)
    column_rows = jnp.arange(piece_rows.shape[0], dtype=jnp.int32)
    same_cluster = (member_ids[:, None] == piece_ids.astype(jnp.int32)[None, :]) & (
        own_rows[:, None] != column_rows[None, :]
    )
    nearest = jnp.max(jnp.where(same_cluster, scores, -1.0), axis=1)
    return jnp.maximum(nearest, -1.0)[None, :]


MEET = ("1o", "2o")
PLACES = 4
SWAP = tuple((f"{place}e", f"{place}o") for place in range(PLACES))
TO_ROOT = (
    (("0e", "0o", "2o", "2e", "3o", "3e", "1o", "1e"),),
    (("0e", "0o"), ("1e~",), ("2e", "1o", "2o"), ("3e", "3o")),
    (("0e", "1o", "1e", "0o"), ("2e", "3o", "2o"), ("3e~",)),
)
BACK = (
    (("0e", "2e", "2o", "0o", "1e", "1o"), ("3e", "3o")),
    (("0e", "0o"), ("1e", "1o", "2e"), ("3e", "2o", "3o")),
    (("0e", "0o"), ("1e~",), ("2e", "2o", "1o", "3e", "3o")),
)


def following(cycles, spot):
    for stops in cycles:
        names = [stop[:2] for stop in stops]
        if spot in names:
            return names[(names.index(spot) + 1) % len(names)]


def wanted(place, parity):
    spot, root = f"{place}{'eo'[parity]}", MEET[parity]
    there = [following(cycles, spot) == root for cycles in TO_ROOT]
    back = [following(cycles, root) == spot for cycles in BACK + (SWAP,)]
    block = 1 + there.index(True) if True in there else 0
    source = 1 + back.index(True) if spot != root else 0
    return source * PLACES + block


def pairs(cycles, batches):
    moves = {}
    for stops in cycles:
        for here, there in zip(stops, stops[1:] + stops[:1]):
            for low in range(0, batches, 2):
                spot = (int(here[0]), low + "eo".index(here[1]))
                other = low ^ 2 if here.endswith("~") else low
                moves[spot] = (int(there[0]), other + "eo".index(there[1]))
    flat = lambda spot: spot[0] * batches + spot[1]
    return sorted((flat(a), flat(b)) for a, b in moves.items())


def travel(array, cycles, batches):
    return lax.ppermute(array, (SPAN, BATCH), pairs(cycles, batches))


GRANT = pltpu.CompilerParams(vmem_limit_bytes=8 << 20)
WHOLE = pl.BlockSpec(memory_space=pltpu.VMEM)


def column_of(row):
    return jnp.transpose(jnp.broadcast_to(row, (8, row.shape[1])))[:, :1]


def best_of(scores, keep):
    return jnp.max(jnp.where(keep, scores, -1.0), axis=0, keepdims=True)


def own_body(rows, out):
    out[...] = normalize(rows[...])


def early_body(guest, own, other, raw, normed, scores):
    count = own.shape[0]
    use_other = jnp.max(guest[...], axis=1, keepdims=True) > 0
    normed[:count, :] = jnp.where(use_other, normalize(other[...]), own[...])
    normed[count:, :] = normalize(raw[...])
    scores[...] = pair_scores(normed[...], normed[...])


def late_body(normed, scores, guest, own_ids, other_ids, early_id, id1, id2, raw1, raw2, out):
    count, half = raw1.shape[0], normed.shape[0]
    first = jnp.where(guest[...] > 0, other_ids[...], own_ids[...])
    early_row = jnp.concatenate([first, early_id[...]], axis=1)
    late_row = jnp.concatenate([id1[...], id2[...]], axis=1)
    early_column, late_column = column_of(early_row), column_of(late_row)
    below = lax.broadcasted_iota(jnp.int32, (half, half), 0)
    beside = lax.broadcasted_iota(jnp.int32, (half, half), 1)
    apart = below != beside
    late = jnp.concatenate([normalize(raw1[...]), normalize(raw2[...])], axis=0)
    cross = pair_scores(normed[...], late)
    cross = jnp.where(early_column == late_row, cross, -1.0)
    inner = best_of(pair_scores(late, late), (late_column == late_row) & apart)
    late_best = jnp.maximum(jnp.max(cross, axis=0, keepdims=True), inner)
    across = jnp.maximum(cross[:, :count], cross[:, count:])
    across = jnp.max(jnp.transpose(across), axis=0, keepdims=True)
    early_best = best_of(scores[...], (early_column == early_row) & apart)
    early_best = jnp.maximum(early_best, across)
    for k, best in enumerate((early_best, late_best)):
        best = jnp.maximum(best, -1.0)
        out[2 * k : 2 * k + 1, :] = best[:, :count]
        out[2 * k + 1 : 2 * k + 2, :] = best[:, count:]


def own_rows(rows):
    return pl.pallas_call(
        own_body,
        out_shape=jax.ShapeDtypeStruct(rows.shape, rows.dtype),
        in_specs=[WHOLE],
        out_specs=WHOLE,
        compiler_params=GRANT,
        name="own_rows",
    )(rows)


def early_pairs(guest, own, other, raw):
    rows, width = 2 * own.shape[0], own.shape[1]
    return pl.pallas_call(
        early_body,
        out_shape=(
            jax.ShapeDtypeStruct((rows, width), jnp.bfloat16),
            jax.ShapeDtypeStruct((rows, rows), jnp.float32),
        ),
        in_specs=[WHOLE] * 4,
        out_specs=(WHOLE, WHOLE),
        compiler_params=GRANT,
        name="early_pairs",
    )(guest, own, other, raw)


def all_results(*args):
    return pl.pallas_call(
        late_body,
        out_shape=jax.ShapeDtypeStruct((PLACES, args[-1].shape[0]), jnp.float32),
        in_specs=[WHOLE] * len(args),
        out_specs=WHOLE,
        compiler_params=GRANT,
        name="all_results",
    )(*args)


def at_root(batches):
    def per_device(embeddings, cluster_ids):
        return whole(embeddings, cluster_ids)

    def whole(embeddings, cluster_ids):
        rows = embeddings[0]
        where_am_i = lax.axis_index(SPAN) * 2 + (lax.axis_index(BATCH) & 1)
        guest = where_am_i == int(MEET[0][0]) * 2 + "eo".index(MEET[0][1])
        guest = jnp.broadcast_to(guest.astype(jnp.int32), cluster_ids.shape)
        inward, outward = TO_ROOT + (SWAP,), BACK + (SWAP,)
        arrived = [travel(rows, c, batches) for c in inward]
        arrived_ids = [travel(cluster_ids, c, batches) for c in inward]
        normed, scores = early_pairs(guest, own_rows(rows), arrived[-1], arrived[0])
        ids = [guest, cluster_ids, arrived_ids[-1]] + arrived_ids[:-1]
        best = all_results(normed, scores, *ids, *arrived[1:-1])
        back = [travel(best, c, batches) for c in outward]
        stack = jnp.concatenate([best] + back, axis=0)
        row = lax.broadcasted_iota(jnp.int32, stack.shape, 0)
        mine = jnp.zeros(stack.shape, jnp.bool_)
        for place in range(PLACES):
            for parity in range(2):
                here = where_am_i == place * 2 + parity
                mine |= here & (row == wanted(place, parity))
        return jnp.max(jnp.where(mine, stack, -1.0), axis=0)[None, :]

    return per_device


def solution(mesh):
    batches = mesh.shape[BATCH]
    line = mesh.shape[SPAN] == PLACES and batches % 4 == 0
    return jax.shard_map(
        at_root(batches) if line else gathered,
        mesh=mesh,
        in_specs=(P(("groups", BATCH), SPAN, None), P(("groups", BATCH), SPAN)),
        out_specs=P(("groups", BATCH), SPAN),
        check_vma=False,
    )
```

```python
import math

import jax
import jax.numpy as jnp
from jax import lax
from jax.experimental import pallas as pl
from jax.experimental.pallas import tpu as pltpu
from jax.sharding import PartitionSpec as P


SPAN = "span"
BATCH = "batch"


def normalize(embeddings):
    values = embeddings.astype(jnp.float32)
    inverse = lax.rsqrt(jnp.mean(values * values, axis=-1, keepdims=True) + 1e-06)
    return (values * inverse * (1.0 / math.sqrt(values.shape[-1]))).astype(jnp.bfloat16)


def pair_scores(left, right):
    return lax.dot_general(
        left, right, (((1,), (1,)), ((), ())), preferred_element_type=jnp.float32
    )


def gathered(embeddings, cluster_ids):
    normed = normalize(embeddings[0])
    member_ids = cluster_ids[0]
    row_count = normed.shape[0]
    own_index = lax.axis_index(SPAN)
    own_rows = own_index * row_count + jnp.arange(row_count, dtype=jnp.int32)
    piece_rows = lax.all_gather(normed, SPAN, axis=0, tiled=True)
    piece_ids = lax.all_gather(member_ids.astype(jnp.bfloat16), SPAN, axis=0, tiled=True)
    scores = pair_scores(normed, piece_rows)
    column_rows = jnp.arange(piece_rows.shape[0], dtype=jnp.int32)
    same_cluster = (member_ids[:, None] == piece_ids.astype(jnp.int32)[None, :]) & (
        own_rows[:, None] != column_rows[None, :]
    )
    nearest = jnp.max(jnp.where(same_cluster, scores, -1.0), axis=1)
    return jnp.maximum(nearest, -1.0)[None, :]


MEET = ("1o", "2o")
PLACES = 4
SWAP = tuple((f"{place}e", f"{place}o") for place in range(PLACES))
TO_ROOT = (
    (("0e", "0o", "2o", "2e", "3o", "3e", "1o", "1e"),),
    (("0e", "0o"), ("1e~",), ("2e", "1o", "2o"), ("3e", "3o")),
    (("0e", "1o", "1e", "0o"), ("2e", "3o", "2o"), ("3e~",)),
)
BACK = (
    (("0e", "2e", "2o", "0o", "1e", "1o"), ("3e", "3o")),
    (("0e", "0o"), ("1e", "1o", "2e"), ("3e", "2o", "3o")),
    (("0e", "0o"), ("1e", "2o", "1o", "3e", "3o", "2e")),
)


def following(cycles, spot):
    for stops in cycles:
        names = [stop[:2] for stop in stops]
        if spot in names:
            return names[(names.index(spot) + 1) % len(names)]


def block_of(spot):
    there = [following(cycles, spot) == MEET["eo".index(spot[1])] for cycles in TO_ROOT]
    return 1 + there.index(True) if True in there else 0


def carried(k):
    ends = [following((BACK + (SWAP,))[k], root) for root in MEET]
    return [block_of(end) if end[1] == "eo"[p] else 0 for p, end in enumerate(ends)]


def turn_of(spot):
    root = MEET["eo".index(spot[1])]
    back = [following(cycles, root) == spot for cycles in BACK + (SWAP,)]
    return 1 + back.index(True) if spot != root else 0


def pairs(cycles, batches):
    moves = {}
    for stops in cycles:
        for here, there in zip(stops, stops[1:] + stops[:1]):
            for low in range(0, batches, 2):
                spot = (int(here[0]), low + "eo".index(here[1]))
                other = low ^ 2 if here.endswith("~") else low
                moves[spot] = (int(there[0]), other + "eo".index(there[1]))
    flat = lambda spot: spot[0] * batches + spot[1]
    return sorted((flat(a), flat(b)) for a, b in moves.items())


def travel(array, cycles, batches):
    return lax.ppermute(array, (SPAN, BATCH), pairs(cycles, batches))


GRANT = pltpu.CompilerParams(vmem_limit_bytes=8 << 20)
WHOLE = pl.BlockSpec(memory_space=pltpu.VMEM)


def column_of(row):
    return jnp.transpose(jnp.broadcast_to(row, (8, row.shape[1])))[:, :1]


def best_of(scores, keep):
    return jnp.max(jnp.where(keep, scores, -1.0), axis=0, keepdims=True)


def own_body(rows, out):
    out[...] = normalize(rows[...])


def early_body(guest, own, other, raw, normed, scores):
    count = own.shape[0]
    use_other = jnp.max(guest[...], axis=1, keepdims=True) > 0
    normed[:count, :] = jnp.where(use_other, normalize(other[...]), own[...])
    normed[count:, :] = normalize(raw[...])
    scores[...] = pair_scores(normed[...], normed[...])


def late_body(normed, scores, guest, own_ids, other_ids, early_id, id1, id2, raw1, raw2, own, *backs):
    count, half = raw1.shape[0], normed.shape[0]
    first = jnp.where(guest[...] > 0, other_ids[...], own_ids[...])
    early_row = jnp.concatenate([first, early_id[...]], axis=1)
    late_row = jnp.concatenate([id1[...], id2[...]], axis=1)
    early_column, late_column = column_of(early_row), column_of(late_row)
    below = lax.broadcasted_iota(jnp.int32, (half, half), 0)
    beside = lax.broadcasted_iota(jnp.int32, (half, half), 1)
    apart = below != beside
    late = jnp.concatenate([normalize(raw1[...]), normalize(raw2[...])], axis=0)
    cross = pair_scores(normed[...], late)
    cross = jnp.where(early_column == late_row, cross, -1.0)
    inner = best_of(pair_scores(late, late), (late_column == late_row) & apart)
    late_best = jnp.maximum(jnp.max(cross, axis=0, keepdims=True), inner)
    across = jnp.maximum(cross[:, :count], cross[:, count:])
    across = jnp.max(jnp.transpose(across), axis=0, keepdims=True)
    early_best = best_of(scores[...], (early_column == early_row) & apart)
    early_best = jnp.maximum(early_best, across)
    blocks = []
    for best in (early_best, late_best):
        best = jnp.maximum(best, -1.0)
        blocks += [best[:, :count], best[:, count:]]
    own[...] = blocks[0]
    for k, back in enumerate(backs):
        even, odd = carried(k)
        back[...] = jnp.where(guest[...] > 0, blocks[even], blocks[odd])


def own_rows(rows):
    return pl.pallas_call(
        own_body,
        out_shape=jax.ShapeDtypeStruct(rows.shape, rows.dtype),
        in_specs=[WHOLE],
        out_specs=WHOLE,
        compiler_params=GRANT,
        name="own_rows",
    )(rows)


def early_pairs(guest, own, other, raw):
    rows, width = 2 * own.shape[0], own.shape[1]
    return pl.pallas_call(
        early_body,
        out_shape=(
            jax.ShapeDtypeStruct((rows, width), jnp.bfloat16),
            jax.ShapeDtypeStruct((rows, rows), jnp.float32),
        ),
        in_specs=[WHOLE] * 4,
        out_specs=(WHOLE, WHOLE),
        compiler_params=GRANT,
        name="early_pairs",
    )(guest, own, other, raw)


def all_results(*args):
    return pl.pallas_call(
        late_body,
        out_shape=(jax.ShapeDtypeStruct((1, args[-1].shape[0]), jnp.float32),) * (1 + PLACES),
        in_specs=[WHOLE] * len(args),
        out_specs=(WHOLE,) * (1 + PLACES),
        compiler_params=GRANT,
        name="all_results",
    )(*args)


def at_root(batches):
    def per_device(embeddings, cluster_ids):
        return whole(embeddings, cluster_ids)

    def whole(embeddings, cluster_ids):
        rows = embeddings[0]
        where_am_i = lax.axis_index(SPAN) * 2 + (lax.axis_index(BATCH) & 1)
        guest = where_am_i == int(MEET[0][0]) * 2 + "eo".index(MEET[0][1])
        guest = jnp.broadcast_to(guest.astype(jnp.int32), cluster_ids.shape)
        turn = jnp.zeros(cluster_ids.shape, jnp.int32)
        for code in range(PLACES * 2):
            spot = f"{code // 2}{'eo'[code % 2]}"
            turn = jnp.where(where_am_i == code, turn_of(spot), turn)
        inward, outward = TO_ROOT + (SWAP,), BACK + (SWAP,)
        arrived = [travel(rows, c, batches) for c in inward]
        arrived_ids = [travel(cluster_ids, c, batches) for c in inward]
        normed, scores = early_pairs(guest, own_rows(rows), arrived[-1], arrived[0])
        ids = [guest, cluster_ids, arrived_ids[-1]] + arrived_ids[:-1]
        result, *sent = all_results(normed, scores, *ids, *arrived[1:-1])
        for k, cycles in enumerate(outward):
            back = travel(sent[k], cycles, batches)
            result = jnp.where(turn == k + 1, back, result)
        return result

    return per_device


def solution(mesh):
    batches = mesh.shape[BATCH]
    line = mesh.shape[SPAN] == PLACES and batches % 4 == 0
    return jax.shard_map(
        at_root(batches) if line else gathered,
        mesh=mesh,
        in_specs=(P(("groups", BATCH), SPAN, None), P(("groups", BATCH), SPAN)),
        out_specs=P(("groups", BATCH), SPAN),
        check_vma=False,
    )
```
